32 devices in a mesh: tm: 4 (over y, x), pts: 8 (over z, core).
Axes of the slice: x: 2, y: 2, z: 4, core: 2. Of those that a mesh axis runs over, the one named last changes fastest.
Arguments:
- orbitals: bfloat16 [8192, 2048], P('pts'), may hold values from -6 to 6
- panel_orbitals: bfloat16 [1024, 2048], P(('tm', 'pts')), may hold values from -0.1796875 to 0.1796875
- band_gap: float32 [2048], replicated, may hold values from 0.1 to 1
- tau_points: float32 [4], replicated, may hold values from 0.1 to 2
- quad_weight: float32 [4], replicated, may hold values from 0.1 to 1
- frequencies: float32 [8], replicated, may hold values from 0.1 to 3
- coulomb: bfloat16 [1024, 1024], P(('tm', 'pts')), may hold values from -0.1875 to 0.1875
Outputs:
- screened: bfloat16 [8, 8192, 1024], P(None, ('pts', 'tm'))
The draws below stay inside these ranges and needn't reach their ends.
All inputs are finite; a program needn't handle non-finite values.
Results may differ from the reference program's by a relative error of at most 0.0056.
Values may be sent and summed in bfloat16 or wider, within the bound.
A program may use at most 64 MiB of HBM per device.

```python
import math
import jax
import jax.numpy as jnp
from jax import lax

NOCC = 512
BANDS = 2048
PANEL = 1024
FREQS = 8
TAUS = 4
NPTS = 8192


def block_scale(key, dims, split, smallest, high):
    gain = 1.0
    for position, parts in split:
        draws = jax.random.uniform(jax.random.fold_in(jax.random.fold_in(key, 6), position), (parts,), jnp.float32, smallest / len(split), high / len(split))
        gain = gain * jnp.repeat(jnp.exp(draws), dims[position] // parts).reshape((-1,) + (1,) * (len(dims) - 1 - position))
    return gain


def gaussian(stream_key, shape, deviation, bound, split=(), dtype=jnp.bfloat16):
    result = jax.random.normal(stream_key, shape, jnp.float32) * deviation
    if len(split) > 0:
        result = block_scale(stream_key, shape, split, -0.22, 0.18) * result
    return jnp.clip(result, min=-bound, max=bound).astype(dtype)


def setup_inputs(seed: int = 0) -> dict:
    seeds = jax.random.split(jax.random.key(seed), 8)
    return {
        "orbitals": gaussian(seeds[0], (NPTS, BANDS), 1.0, 6.0, ((0, 8),)),
        "panel_orbitals": gaussian(seeds[1], (PANEL, BANDS), 0.03, 0.1796875, ((0, 32),)),
        "band_gap": jnp.clip(jnp.exp(jax.random.uniform(seeds[2], (BANDS,), jnp.float32, math.log(0.1), math.log(1.0))), 0.1, 1.0),
        "tau_points": jnp.clip(jnp.exp(jax.random.uniform(seeds[3], (TAUS,), jnp.float32, math.log(0.1), math.log(2.0))), 0.1, 2.0),
        "quad_weight": jnp.clip(jnp.exp(jax.random.uniform(seeds[4], (TAUS,), jnp.float32, math.log(0.1), math.log(1.0))), 0.1, 1.0),
        "frequencies": jnp.clip(jnp.exp(jax.random.uniform(seeds[5], (FREQS,), jnp.float32, math.log(0.1), math.log(3.0))), 0.1, 3.0),
        "coulomb": gaussian(seeds[6], (PANEL, PANEL), PANEL ** -0.5, 0.1875, ((0, 32),)),
    }


def contract(left, right):
    return lax.dot_general(left, right, (((1,), (1,)), ((), ())), preferred_element_type=jnp.float32)


def reference(orbitals, panel_orbitals, band_gap, tau_points, quad_weight, frequencies, coulomb):
    cosines = quad_weight[None, :] * jnp.cos(frequencies[:, None] * tau_points[None, :])
    occ_rows = orbitals[:, :NOCC]
    vir_rows = orbitals[:, NOCC:]
    layers = []
    for slot in range(TAUS):
        decay = jnp.exp(-band_gap * tau_points[slot])
        scaled = (panel_orbitals.astype(jnp.float32) * decay[None, :]).astype(jnp.bfloat16)
        green_occ = contract(occ_rows, scaled[:, :NOCC])
        green_vir = contract(vir_rows, scaled[:, NOCC:])
        layers.append((-(green_occ * green_vir)).astype(jnp.bfloat16))
    polar = jnp.stack(layers)
    flat = polar.reshape(TAUS, NPTS * PANEL).astype(jnp.float32)
    transformed = jnp.dot(cosines, flat, precision=lax.Precision.HIGHEST).astype(jnp.bfloat16)
    transformed = transformed.reshape(FREQS * NPTS, PANEL)
    screened = jnp.dot(transformed, coulomb, preferred_element_type=jnp.float32).astype(jnp.bfloat16)
    return screened.reshape(FREQS, NPTS, PANEL)
```

```python
import jax
import jax.numpy as jnp
from jax import lax
from jax.sharding import PartitionSpec as P

NOCC = 512


def contract(left, right):
    return lax.dot_general(
        left, right, (((1,), (1,)), ((), ())), preferred_element_type=jnp.float32
    )


def shards(orbitals, panel_orbitals, band_gap, tau_points, quad_weight, frequencies, coulomb):
    times = tau_points.shape[0]
    rows = orbitals.shape[0] // lax.axis_size("tm")
    own = lax.dynamic_slice_in_dim(orbitals, lax.axis_index("tm") * rows, rows)
    decay = jnp.exp(-band_gap[None, :] * tau_points[:, None])
    scaled = (own.astype(jnp.float32)[None] * decay[:, None, :]).astype(jnp.bfloat16)
    scaled = scaled.reshape(times * rows, -1)
    panel = lax.all_gather(panel_orbitals, ("tm", "pts"), axis=0, tiled=True)
    block = lax.all_gather(coulomb, ("tm", "pts"), axis=0, tiled=True)
    green_occ = contract(scaled[:, :NOCC], panel[:, :NOCC])
    green_vir = contract(scaled[:, NOCC:], panel[:, NOCC:])
    polar = (-(green_occ * green_vir)).astype(jnp.bfloat16)
    product = jnp.dot(polar, block, preferred_element_type=jnp.float32)
    product = product.reshape(times, rows, -1)
    cosines = quad_weight[None, :] * jnp.cos(frequencies[:, None] * tau_points[None, :])
    total = cosines[:, 0, None, None] * product[None, 0]
    for t in range(1, times):
        total = total + cosines[:, t, None, None] * product[None, t]
    return total.astype(jnp.bfloat16)


def solution(mesh):
    placed = (P("pts", None), P(("tm", "pts"), None), P(), P(), P(), P(), P(("tm", "pts"), None))
    return jax.shard_map(
        shards, mesh=mesh, in_specs=placed, out_specs=P(None, ("pts", "tm"), None), check_vma=False
    )
```

```python
import functools
import jax
import jax.numpy as jnp
from jax import lax
from jax.experimental import pallas as pl
from jax.experimental.pallas import tpu as pltpu
from jax.sharding import PartitionSpec as P

NOCC = 512
MESH = pl.DeviceIdType.MESH
DIRS = 7


def when(valid, run):
    if valid is True:
        run()
    elif valid is not False:
        pl.when(valid)(run)


def both(a, b):
    if a is True:
        return b
    if b is True:
        return a
    if a is False or b is False:
        return False
    return jnp.logical_and(a, b)


class Line:
    def __init__(self, at, size):
        self.at, self.size = at, size
        if size == 1:
            self.sends, self.arrivals, self.peers = [], [], 0
        elif size == 2:
            other = 1 - at
            self.peers = 1
            self.sends = [(0, other, True)]
            self.arrivals = [(other, True, [])]
        elif size <= 4:
            down, up = at > 0, at < size - 1
            self.peers = lax.div(at + size - 1, size) + lax.div(2 * size - 2 - at, size)
            self.sends = [(0, at - 1, down), (1, at + 1, up)]
            self.arrivals = []
            for far in range(1, size):
                self.arrivals.append((at - far, at >= far, [(1, at + 1, up)]))
                self.arrivals.append((at + far, at < size - far, [(0, at - 1, down)]))
        else:
            before, after = lax.rem(at + size - 1, size), lax.rem(at + 1, size)
            self.sends = [(0, before, True), (1, after, True)]
            self.peers = 2
            self.arrivals = []
            ups, downs = size // 2, (size - 1) // 2
            for far in range(1, ups + 1):
                on = [(1, after, True)] if far < ups else []
                self.arrivals.append((lax.rem(at + size - far, size), True, on))
                if far <= downs:
                    on = [(0, before, True)] if far < downs else []
                    self.arrivals.append((lax.rem(at + far, size), True, on))


def gather_kernel(
    sizes, panel_ref, coulomb_ref, orbitals_ref, decay_ref, polar_ref, block_ref,
    full, own, lhs, local_sem, ici_sem, par_sem, snd_sem,
):
    ny, nx, nz = sizes
    tm, pts = lax.axis_index("tm"), lax.axis_index("pts")
    core = lax.rem(pts, 2)
    here = {"y": lax.div(tm, nx), "x": lax.rem(tm, nx), "z": lax.div(pts, 2)}
    lines = {"y": Line(here["y"], ny), "x": Line(here["x"], nx), "z": Line(here["z"], nz)}
    base = {"y": 1, "x": 3, "z": 5}
    shard = panel_ref.shape[0]
    half = shard // 2
    bands = panel_ref.shape[1]
    times = decay_ref.shape[0]
    rows = own.shape[0]
    orders = (("z", "x", "y"), ("z", "y", "x"))

    def device(at, on):
        return {"tm": at["y"] * nx + at["x"], "pts": at["z"] * 2 + on}

    def chip(at):
        return (at["y"] * nx + at["x"]) * nz + at["z"]

    def piece(stream, at, on):
        start = (chip(at) * 2 + on) * shard + stream * half
        return full.at[pl.ds(pl.multiple_of(start, half), half), :]

    def ici_copy(stream, at, axis, slot, to):
        target = dict(here)
        target[axis] = to
        return pltpu.make_async_remote_copy(
            src_ref=piece(stream, at, core), dst_ref=piece(stream, at, core),
            send_sem=snd_sem.at[stream, chip(at), base[axis] + slot],
            recv_sem=ici_sem.at[stream, chip(at)],
            device_id=device(target, core), device_id_type=MESH,
        )

    def partner_copy(stream, at, on):
        return pltpu.make_async_remote_copy(
            src_ref=piece(stream, at, on), dst_ref=piece(stream, at, on),
            send_sem=snd_sem.at[stream, chip(at), 0],
            recv_sem=par_sem.at[stream, chip(at)],
            device_id=device(here, 1 - core), device_id_type=MESH,
        )

    own_orbitals = pltpu.make_async_copy(
        orbitals_ref.at[pl.ds(pl.multiple_of(tm * rows, rows), rows), :], own, local_sem.at[0])
    mine = (chip(here) * 2 + core) * shard
    mine_rows = pl.ds(pl.multiple_of(mine, shard), shard)
    own_panel = pltpu.make_async_copy(panel_ref, full.at[mine_rows, :bands], local_sem.at[1])
    own_coulomb = pltpu.make_async_copy(coulomb_ref, full.at[mine_rows, bands:], local_sem.at[2])
    own_panel.start()
    own_coulomb.start()
    own_orbitals.start()

    barrier = pltpu.get_barrier_semaphore()
    peers = [(device(here, 1 - core), True)]
    for axis in "yxz":
        for _, to, valid in lines[axis].sends:
            target = dict(here)
            target[axis] = to
            peers.append((device(target, core), valid))
    for to, valid in peers:
        when(valid, lambda to=to: pl.semaphore_signal(barrier, inc=1, device_id=to, device_id_type=MESH))
    greeted = 1
    for line in lines.values():
        greeted = greeted + line.peers
    pl.semaphore_wait(barrier, greeted)

    own_panel.wait()
    own_coulomb.wait()

    sent = []

    def forward(stream, at, valid, hops):
        for axis, slot, to, ok in hops:
            when(ok, lambda axis=axis, slot=slot, to=to: ici_copy(stream, at, axis, slot, to).start())
        partner_copy(stream, at, core).start()

    def note(stream, at, valid, hops):
        for axis, slot, to, ok in hops:
            sent.append((stream, at, axis, slot, to, both(valid, ok)))

    def later(order, place):
        return [(axis, slot, to, ok) for axis in order[place:] for slot, to, ok in lines[axis].sends]

    def take(stream, at, valid, order, place, on):
        hops = [(order[place], slot, to, ok) for slot, to, ok in on] + later(order, place + 1)

        def run():
            ici_copy(stream, at, order[place], 0, here[order[place]]).wait_recv()
            forward(stream, at, valid, hops)

        note(stream, at, valid, hops)
        when(valid, run)

    for stream, order in enumerate(orders):
        note(stream, dict(here), True, later(order, 0))
        forward(stream, dict(here), True, later(order, 0))

    own_orbitals.wait()
    lanes = 512

    def scale(t, carry):
        for start in range(0, bands, lanes):
            cut = slice(start, start + lanes)
            value = own[:, cut].astype(jnp.float32) * decay_ref[pl.ds(t, 1), cut]
            lhs[pl.ds(pl.multiple_of(t * rows, rows), rows), cut] = value.astype(jnp.bfloat16)
        return carry

    lax.fori_loop(0, times, scale, 0)

    def with_axis(at, axis, to):
        moved = dict(at)
        moved[axis] = to
        return moved

    first = [(dict(here), True)]
    for to, valid, on in lines["z"].arrivals:
        at = with_axis(here, "z", to)
        for stream, order in enumerate(orders):
            take(stream, at, valid, order, 0, on)
        first.append((at, valid))

    columns = 2 * nz * shard

    def column_ready(y, x):
        for z in range(nz):
            at = {"y": y, "x": x, "z": z}
            for stream in range(2):
                partner_copy(stream, at, 1 - core).wait_recv()

    def compute(y, x):
        column_ready(y, x)
        group = y * nx + x
        cut = pl.ds(pl.multiple_of(group * columns, columns), columns)
        pltpu.make_async_copy(full.at[cut, bands:], block_ref.at[cut, :], local_sem.at[3 + group]).start()
        contract = (((1,), (1,)), ((), ()))

        def one(t, carry):
            mine = pl.ds(pl.multiple_of(t * rows, rows), rows)
            occ = lax.dot_general(lhs[mine, :NOCC], full[cut, :NOCC], contract,
                                  preferred_element_type=jnp.float32)
            vir = lax.dot_general(lhs[mine, NOCC:], full[cut, NOCC:bands], contract,
                                  preferred_element_type=jnp.float32)
            polar_ref[mine, cut] = (-(occ * vir)).astype(jnp.bfloat16)
            return carry

        lax.fori_loop(0, times, one, 0)

    compute(here["y"], here["x"])

    arrivals = [(axis, *entry) for axis in ("x", "y") for entry in lines[axis].arrivals]
    for at0, valid0 in first:
        for axis, to, valid, on in arrivals:
            at = with_axis(at0, axis, to)
            for stream, order in enumerate(orders):
                take(stream, at, both(valid0, valid), order, order.index(axis), on)
    for axis, to, valid, on in arrivals:
        when(valid, lambda axis=axis, to=to: compute(
            to if axis == "y" else here["y"], to if axis == "x" else here["x"]))
    for at0, valid0 in first:
        for y, valid1, on_y in lines["y"].arrivals:
            for x, valid2, on_x in lines["x"].arrivals:
                at = with_axis(with_axis(at0, "y", y), "x", x)
                valid = both(valid0, both(valid1, valid2))
                take(0, at, valid, orders[0], 2, on_y)
                take(1, at, valid, orders[1], 2, on_x)
    for y, valid1, _ in lines["y"].arrivals:
        for x, valid2, _ in lines["x"].arrivals:
            when(both(valid1, valid2), lambda y=y, x=x: compute(y, x))

    for stream, at, axis, slot, to, valid in sent:
        when(valid, lambda stream=stream, at=at, axis=axis, slot=slot, to=to:
             ici_copy(stream, at, axis, slot, to).wait_send())
    for y in range(ny):
        for x in range(nx):
            for z in range(nz):
                for stream in range(2):
                    partner_copy(stream, {"y": y, "x": x, "z": z}, core).wait_send()
    group = pl.ds(0, columns)
    for slot in range(ny * nx):
        pltpu.make_async_copy(full.at[group, bands:], block_ref.at[group, :], local_sem.at[3 + slot]).wait()


def finish_kernel(times, freqs, cosines_ref, polar_ref, block_ref, out_ref):
    parts = [
        jnp.dot(polar_ref[t], block_ref[...], preferred_element_type=jnp.float32) for t in range(times)
    ]
    for k in range(freqs):
        total = cosines_ref[k, 0] * parts[0]
        for t in range(1, times):
            total = total + cosines_ref[k, t] * parts[t]
        out_ref[k] = total.astype(out_ref.dtype)


def shards(sizes, orbitals, panel_orbitals, band_gap, tau_points, quad_weight, frequencies, coulomb):
    times = tau_points.shape[0]
    freqs = frequencies.shape[0]
    groups = lax.axis_size("tm")
    devices = groups * lax.axis_size("pts")
    bands = orbitals.shape[1]
    rows = orbitals.shape[0] // groups
    shard = panel_orbitals.shape[0]
    panel = shard * devices
    width = coulomb.shape[1]
    chips = devices // 2
    decay = jnp.exp(-band_gap[None, :] * tau_points[:, None])
    cosines = quad_weight[None, :] * jnp.cos(frequencies[:, None] * tau_points[None, :])
    hbm = pl.BlockSpec(memory_space=pl.ANY)
    vmem = pl.BlockSpec(memory_space=pltpu.VMEM)
    polar, block = pl.pallas_call(
        functools.partial(gather_kernel, sizes),
        out_shape=(
            jax.ShapeDtypeStruct((times * rows, panel), jnp.bfloat16),
            jax.ShapeDtypeStruct((panel, width), jnp.bfloat16),
        ),
        in_specs=[hbm, hbm, hbm, vmem],
        out_specs=(vmem, hbm),
        scratch_shapes=[
            pltpu.VMEM((panel, bands + width), jnp.bfloat16),
            pltpu.VMEM((rows, bands), jnp.bfloat16),
            pltpu.VMEM((times * rows, bands), jnp.bfloat16),
            pltpu.SemaphoreType.DMA((3 + groups,)),
            pltpu.SemaphoreType.DMA((2, chips)),
            pltpu.SemaphoreType.DMA((2, chips)),
            pltpu.SemaphoreType.DMA((2, chips, DIRS)),
        ],
        compiler_params=pltpu.CompilerParams(
            collective_id=0, has_side_effects=True, vmem_limit_bytes=48 * 1024 * 1024
        ),
        name="gather_polar",
    )(panel_orbitals, coulomb, orbitals, decay)
    tile = min(rows, 128)
    wide = min(width, 256)
    return pl.pallas_call(
        functools.partial(finish_kernel, times, freqs),
        grid=(rows // tile, width // wide),
        out_shape=jax.ShapeDtypeStruct((freqs, rows, width), jnp.bfloat16),
        in_specs=[
            pl.BlockSpec(memory_space=pltpu.SMEM),
            pl.BlockSpec((times, tile, panel), lambda i, j: (0, i, 0)),
            pl.BlockSpec((panel, wide), lambda i, j: (0, j)),
        ],
        out_specs=pl.BlockSpec((freqs, tile, wide), lambda i, j: (0, i, j)),
        compiler_params=pltpu.CompilerParams(vmem_limit_bytes=48 * 1024 * 1024),
        name="screen",
    )(cosines, polar.reshape(times, rows, panel), block)


def solution(mesh):
    groups, points = mesh.shape["tm"], mesh.shape["pts"]
    sizes = (groups // 2, 2, points // 2)
    placed = (P("pts", None), P(("tm", "pts"), None), P(), P(), P(), P(), P(("tm", "pts"), None))
    return jax.shard_map(
        functools.partial(shards, sizes), mesh=mesh, in_specs=placed,
        out_specs=P(None, ("pts", "tm"), None), check_vma=False,
    )
```

```python
import functools
import jax
import jax.numpy as jnp
from jax import lax
from jax.experimental import pallas as pl
from jax.experimental.pallas import tpu as pltpu
from jax.sharding import PartitionSpec as P

NOCC = 512
MESH = pl.DeviceIdType.MESH
LANES = 128


def when(valid, run):
    if valid is True:
        run()
    elif valid is not False:
        pl.when(valid)(run)


def both(a, b):
    if a is True:
        return b
    if b is True:
        return a
    if a is False or b is False:
        return False
    return jnp.logical_and(a, b)


class Line:
    def __init__(self, at, size):
        self.at, self.size = at, size
        if size == 1:
            self.sends, self.arrivals, self.peers = [], [], 0
        elif size == 2:
            other = 1 - at
            self.peers = 1
            self.sends = [(0, other, True)]
            self.arrivals = [(other, True, [])]
        elif size <= 4:
            down, up = at > 0, at < size - 1
            self.peers = lax.div(at + size - 1, size) + lax.div(2 * size - 2 - at, size)
            self.sends = [(0, at - 1, down), (1, at + 1, up)]
            self.arrivals = []
            for far in range(1, size):
                self.arrivals.append((at - far, at >= far, [(1, at + 1, up)]))
                self.arrivals.append((at + far, at < size - far, [(0, at - 1, down)]))
        else:
            before, after = lax.rem(at + size - 1, size), lax.rem(at + 1, size)
            self.sends = [(0, before, True), (1, after, True)]
            self.peers = 2
            self.arrivals = []
            ups, downs = size // 2, (size - 1) // 2
            for far in range(1, ups + 1):
                on = [(1, after, True)] if far < ups else []
                self.arrivals.append((lax.rem(at + size - far, size), True, on))
                if far <= downs:
                    on = [(0, before, True)] if far < downs else []
                    self.arrivals.append((lax.rem(at + far, size), True, on))


def gather_kernel(
    sizes, panel_ref, coulomb_ref, orbitals_ref, band_ref, tau_ref, weight_ref, freq_ref, sum_ref, cos_ref,
    panel, block, own, lhs, local_sem, ici_sem, par_sem, snd_sem,
):
    ny, nx, nz = sizes
    tm, pts = lax.axis_index("tm"), lax.axis_index("pts")
    core = lax.rem(pts, 2)
    here = {"y": lax.div(tm, nx), "x": lax.rem(tm, nx), "z": lax.div(pts, 2)}
    lines = {"y": Line(here["y"], ny), "x": Line(here["x"], nx), "z": Line(here["z"], nz)}
    base = {"y": 1, "x": 1 + slots(ny), "z": 1 + slots(ny) + slots(nx)}
    shard = panel_ref.shape[0]
    half = shard // 2
    bands = panel_ref.shape[1]
    times = tau_ref.shape[0]
    freqs = freq_ref.shape[0]
    rows = own.shape[0]
    streams = (
        (panel, 0, ("x", "z", "y")), (panel, 1, ("y", "z", "x")),
        (block, 0, ("z", "x", "y")), (block, 1, ("z", "y", "x")),
    )
    kinds = range(len(streams))

    def device(at, on):
        return {"tm": at["y"] * nx + at["x"], "pts": at["z"] * 2 + on}

    def chip(at):
        return (at["y"] * nx + at["x"]) * nz + at["z"]

    def piece(kind, at, on):
        array, part, _ = streams[kind]
        start = (chip(at) * 2 + on) * shard + part * half
        return array.at[pl.ds(pl.multiple_of(start, half), half), :]

    def moved(at, axis, to):
        other = dict(at)
        other[axis] = to
        return other

    def ici_copy(kind, at, axis, slot, to):
        return pltpu.make_async_remote_copy(
            src_ref=piece(kind, at, core), dst_ref=piece(kind, at, core),
            send_sem=snd_sem.at[kind, chip(at), base[axis] + slot],
            recv_sem=ici_sem.at[kind, chip(at)],
            device_id=device(moved(here, axis, to), core), device_id_type=MESH,
        )

    def partner_copy(kind, at, on):
        return pltpu.make_async_remote_copy(
            src_ref=piece(kind, at, on), dst_ref=piece(kind, at, on),
            send_sem=snd_sem.at[kind, chip(at), 0],
            recv_sem=par_sem.at[kind, chip(at)],
            device_id=device(here, 1 - core), device_id_type=MESH,
        )

    own_orbitals = pltpu.make_async_copy(
        orbitals_ref.at[pl.ds(pl.multiple_of(tm * rows, rows), rows), :], own, local_sem.at[0])
    mine = (chip(here) * 2 + core) * shard
    mine_rows = pl.ds(pl.multiple_of(mine, shard), shard)
    own_panel = pltpu.make_async_copy(panel_ref, panel.at[mine_rows, :], local_sem.at[1])
    own_coulomb = pltpu.make_async_copy(coulomb_ref, block.at[mine_rows, :], local_sem.at[2])
    own_panel.start()
    own_coulomb.start()
    own_orbitals.start()

    barrier = pltpu.get_barrier_semaphore()
    peers = [(device(here, 1 - core), True)]
    greeted = 1
    for axis, line in lines.items():
        greeted = greeted + line.peers
        for _, to, valid in line.sends:
            peers.append((device(moved(here, axis, to), core), valid))
    for to, valid in peers:
        when(valid, lambda to=to: pl.semaphore_signal(barrier, inc=1, device_id=to, device_id_type=MESH))
    pl.semaphore_wait(barrier, greeted)

    own_panel.wait()
    own_coulomb.wait()

    sent = []

    def forward(kind, at, hops):
        for axis, slot, to, ok in hops:
            when(ok, lambda axis=axis, slot=slot, to=to: ici_copy(kind, at, axis, slot, to).start())
        partner_copy(kind, at, core).start()

    def note(kind, at, valid, hops):
        for axis, slot, to, ok in hops:
            sent.append((kind, at, axis, slot, to, both(valid, ok)))

    def later(order, place):
        return [(axis, slot, to, ok) for axis in order[place:] for slot, to, ok in lines[axis].sends]

    def take(kind, entries):
        order = streams[kind][2]
        place = max(order.index(axis) for axis in entries)
        at, valid = dict(here), True
        for axis, (to, ok, _) in entries.items():
            at[axis] = to
            valid = both(valid, ok)
        last = order[place]
        hops = [(last, slot, to, ok) for slot, to, ok in entries[last][2]] + later(order, place + 1)

        def run():
            ici_copy(kind, at, last, 0, here[last]).wait_recv()
            forward(kind, at, hops)

        note(kind, at, valid, hops)
        when(valid, run)

    for kind in kinds:
        hops = later(streams[kind][2], 0)
        note(kind, dict(here), True, hops)
        forward(kind, dict(here), hops)

    own_orbitals.wait()
    gap = band_ref[...]
    for t in range(times):
        decay = jnp.exp(-gap * tau_ref[t])
        cut = slice(t * rows, (t + 1) * rows)
        for start in range(0, bands, 512):
            wide = slice(start, start + 512)
            value = own[:, wide].astype(jnp.float32) * decay[:, wide]
            lhs[cut, wide] = value.astype(jnp.bfloat16)
    place = lax.broadcasted_iota(jnp.int32, (freqs, LANES), 0)
    freq = jnp.zeros((freqs, LANES), jnp.float32)
    for k in range(freqs):
        freq = jnp.where(place == k, freq_ref[k], freq)
    for t in range(times):
        cos_ref[t] = weight_ref[t] * jnp.cos(freq * tau_ref[t])

    columns = 2 * nz * shard
    work = []

    def compute(y, x, valid, fresh):
        group = y * nx + x
        cut = pl.ds(pl.multiple_of(group * columns, columns), columns)
        contract = (((1,), (1,)), ((), ()))

        def one(t):
            if t == 0:
                for z in range(nz):
                    for kind in kinds:
                        partner_copy(kind, {"y": y, "x": x, "z": z}, 1 - core).wait_recv()
            mine = slice(t * rows, (t + 1) * rows)
            occ = lax.dot_general(lhs[mine, :NOCC], panel[cut, :NOCC], contract,
                                  preferred_element_type=jnp.float32)
            vir = lax.dot_general(lhs[mine, NOCC:], panel[cut, NOCC:], contract,
                                  preferred_element_type=jnp.float32)
            polar = (-(occ * vir)).astype(jnp.bfloat16)
            term = jnp.dot(polar, block[cut, :], preferred_element_type=jnp.float32)
            if fresh:
                sum_ref[mine, :] = term
            else:
                sum_ref[mine, :] += term

        for t in range(times):
            work.append((valid, functools.partial(one, t)))

    def step():
        if work:
            valid, run = work.pop(0)
            when(valid, run)

    def take_sides(entries):
        for kind in kinds:
            for axis in ("x", "y"):
                for entry in lines[axis].arrivals:
                    take(kind, {**entries, axis: entry})

    along = lines["z"].arrivals
    batches = [along[i:i + 2] for i in range(0, len(along), 2)]
    ahead = [{}]
    for batch in batches:
        for entry in batch:
            for kind in kinds:
                take(kind, {"z": entry})
        for entries in ahead:
            take_sides(entries)
        ahead = [{"z": entry} for entry in batch]
    compute(here["y"], here["x"], True, True)
    for entries in ahead:
        take_sides(entries)
    step()
    for axis in ("x", "y"):
        for to, valid, _ in lines[axis].arrivals:
            compute(to if axis == "y" else here["y"], to if axis == "x" else here["x"], valid, False)
    steps = -(-len(work) // (1 + len(along)))
    for entries in [{}] + [{"z": entry} for entry in along]:
        for y in lines["y"].arrivals:
            for x in lines["x"].arrivals:
                for kind in kinds:
                    take(kind, {**entries, "y": y, "x": x})
        for _ in range(steps):
            step()
    for y, valid1, _ in lines["y"].arrivals:
        for x, valid2, _ in lines["x"].arrivals:
            compute(y, x, both(valid1, valid2), False)
    while work:
        step()

    for kind, at, axis, slot, to, valid in sent:
        when(valid, lambda kind=kind, at=at, axis=axis, slot=slot, to=to:
             ici_copy(kind, at, axis, slot, to).wait_send())
    for y in range(ny):
        for x in range(nx):
            for z in range(nz):
                for kind in kinds:
                    partner_copy(kind, {"y": y, "x": x, "z": z}, core).wait_send()


def finish_kernel(times, freqs, cos_ref, sum_ref, out_ref):
    tile = 16
    weights = [[cos_ref[t, k:k + 1, 0:1] for t in range(times)] for k in range(freqs)]

    def some(i, carry):
        cut = pl.ds(pl.multiple_of(i * tile, tile), tile)
        parts = [sum_ref[t, cut, :] for t in range(times)]
        for k in range(freqs):
            total = weights[k][0] * parts[0]
            for t in range(1, times):
                total = total + weights[k][t] * parts[t]
            out_ref[k, cut, :] = total.astype(out_ref.dtype)
        return carry

    lax.fori_loop(0, sum_ref.shape[1] // tile, some, 0)


def slots(size):
    return min(size - 1, 2)


def shards(sizes, orbitals, panel_orbitals, band_gap, tau_points, quad_weight, frequencies, coulomb):
    times = tau_points.shape[0]
    freqs = frequencies.shape[0]
    groups = lax.axis_size("tm")
    devices = groups * lax.axis_size("pts")
    bands = orbitals.shape[1]
    rows = orbitals.shape[0] // groups
    panel = panel_orbitals.shape[0] * devices
    width = coulomb.shape[1]
    chips = devices // 2
    hbm = pl.BlockSpec(memory_space=pltpu.HBM)
    vmem = pl.BlockSpec(memory_space=pltpu.VMEM)
    smem = pl.BlockSpec(memory_space=pltpu.SMEM)
    sums, cosines = pl.pallas_call(
        functools.partial(gather_kernel, sizes),
        out_shape=(
            jax.ShapeDtypeStruct((times * rows, width), jnp.float32),
            jax.ShapeDtypeStruct((times, freqs, LANES), jnp.float32),
        ),
        in_specs=[hbm, hbm, hbm, vmem, smem, smem, smem],
        out_specs=(vmem, vmem),
        scratch_shapes=[
            pltpu.VMEM((panel, bands), jnp.bfloat16),
            pltpu.VMEM((panel, width), jnp.bfloat16),
            pltpu.VMEM((rows, bands), jnp.bfloat16),
            pltpu.VMEM((times * rows, bands), jnp.bfloat16),
            pltpu.SemaphoreType.DMA((3,)),
            pltpu.SemaphoreType.DMA((4, chips)),
            pltpu.SemaphoreType.DMA((4, chips)),
            pltpu.SemaphoreType.DMA((4, chips, 1 + sum(slots(size) for size in sizes))),
        ],
        compiler_params=pltpu.CompilerParams(
            collective_id=0, has_side_effects=True, vmem_limit_bytes=62824448
        ),
        name="gather_sum",
    )(panel_orbitals, coulomb, orbitals, band_gap.reshape(1, bands), tau_points, quad_weight, frequencies)
    tile = min(rows, 64)
    return pl.pallas_call(
        functools.partial(finish_kernel, times, freqs),
        grid=(rows // tile,),
        out_shape=jax.ShapeDtypeStruct((freqs, rows, width), jnp.bfloat16),
        in_specs=[
            pl.BlockSpec((times, freqs, LANES), lambda i: (0, 0, 0)),
            pl.BlockSpec((times, tile, width), lambda i: (0, i, 0)),
        ],
        out_specs=pl.BlockSpec((freqs, tile, width), lambda i: (0, i, 0)),
        compiler_params=pltpu.CompilerParams(vmem_limit_bytes=62824448),
        name="finish",
    )(cosines, sums.reshape(times, rows, width))


def contract(left, right):
    return lax.dot_general(
        left, right, (((1,), (1,)), ((), ())), preferred_element_type=jnp.float32
    )


def many_shards(orbitals, panel_orbitals, band_gap, tau_points, quad_weight, frequencies, coulomb):
    times = tau_points.shape[0]
    rows = orbitals.shape[0] // lax.axis_size("tm")
    own = lax.dynamic_slice_in_dim(orbitals, lax.axis_index("tm") * rows, rows)
    decay = jnp.exp(-band_gap[None, :] * tau_points[:, None])
    scaled = (own.astype(jnp.float32)[None] * decay[:, None, :]).astype(jnp.bfloat16)
    scaled = scaled.reshape(times * rows, -1)
    panel = lax.all_gather(panel_orbitals, ("tm", "pts"), axis=0, tiled=True)
    block = lax.all_gather(coulomb, ("tm", "pts"), axis=0, tiled=True)
    green_occ = contract(scaled[:, :NOCC], panel[:, :NOCC])
    green_vir = contract(scaled[:, NOCC:], panel[:, NOCC:])
    polar = (-(green_occ * green_vir)).astype(jnp.bfloat16)
    product = jnp.dot(polar, block, preferred_element_type=jnp.float32)
    product = product.reshape(times, rows, -1)
    cosines = quad_weight[None, :] * jnp.cos(frequencies[:, None] * tau_points[None, :])
    total = cosines[:, 0, None, None] * product[None, 0]
    for t in range(1, times):
        total = total + cosines[:, t, None, None] * product[None, t]
    return total.astype(jnp.bfloat16)


def solution(mesh):
    groups, points = mesh.shape["tm"], mesh.shape["pts"]
    sizes = (groups // 2, 2, points // 2)
    placed = (P("pts", None), P(("tm", "pts"), None), P(), P(), P(), P(), P(("tm", "pts"), None))
    local = functools.partial(shards, sizes) if groups * points <= 32 else many_shards
    return jax.shard_map(
        local, mesh=mesh, in_specs=placed,
        out_specs=P(None, ("pts", "tm"), None), check_vma=False,
    )
```
